32 devices in a mesh: groups: 2 (over x), tm: 16 (over z, y, core).
Axes of the slice: x: 2, y: 2, z: 4, core: 2. Of those that a mesh axis runs over, the one named last changes fastest.
Arguments:
- records: bfloat16 [384, 4096], P('groups', 'tm'), parts along dimension 0, may hold values from -6 to 6
- bank: bfloat16 [256, 384, 240], P('tm', 'groups'), parts along dimension 1, may hold values from -6 to 6
- plan: int32 [6], P('groups'), parts along dimension 0, may hold values from 0 to 15
- template_ids: int32 [6, 2], P('groups'), parts along dimension 0, may hold values from 0 to 15
- channel_mask: int32 [384], P('groups'), parts along dimension 0, may hold values 0 or 1
Outputs:
- detection: float32 [6, 2, 4096], P('groups', None, 'tm'), parts along dimension 0
The draws below stay inside these ranges and needn't reach their ends.
There are 2 independent parts, one for each index of `groups`. The reference program is written for one: setup_inputs(seed, part) draws one part's arguments, and reference() takes and returns one part's arrays. A program takes and returns all parts, laid end to end along the dimension named above; each array names one. Nothing has to cross between parts.
Inputs may be any that keep to these rules, and one draw needn't show every extreme that they name: `plan`: the index of tm that holds a step's templates. `template_ids`: slots within the owner's 16 templates.
All inputs are finite; a program needn't handle non-finite values.
Results may differ from the reference program's by a relative error of at most 0.0003.
Values may be sent and summed in bfloat16 or wider, within the bound.
A program may use at most 64 MiB of HBM per device.

```python
import jax
import jax.numpy as jnp
from jax import lax

C = 192
L = 240
K = 2
STEPS = 3
SLOTS = 16
TOTAL = 4096
BANK = 256
N_TM = 16


def place_ends(values, stream_key, low, largest):
    longest = values.shape.index(max(values.shape))
    spots = []
    for shift in (0, 1):
        where = [jax.random.randint(jax.random.fold_in(stream_key, axis), (), 0, length) for axis, length in enumerate(values.shape)]
        where[longest] = (where[longest] + shift) % values.shape[longest]
        spots.append(tuple(where))
    return values.at[spots[0]].set(low).at[spots[1]].set(largest)


def steps_of(stream_key, shape, cuts, least, high):
    def one(position, blocks):
        steps = jax.random.uniform(jax.random.fold_in(jax.random.fold_in(stream_key, 6), position), (blocks,), jnp.float32, least / len(cuts), high / len(cuts))
        return jnp.repeat(jnp.exp(steps), shape[position] // blocks).reshape((-1,) + (1,) * (len(shape) - position - 1))

    loudness = one(*cuts[0])
    for cut in cuts[1:]:
        loudness = loudness * one(*cut)
    return loudness


def noise(own_key, dims, width, reach, pieces=(), held_as=jnp.bfloat16):
    values = width * jax.random.normal(own_key, dims, jnp.float32)
    if pieces:
        values = values * steps_of(own_key, dims, pieces, -0.22, 0.18)
    return jnp.clip(values, -reach, reach).astype(held_as)


def setup_inputs(seed: int = 0, part: int = 0) -> dict:
    key_list = jax.random.split(jax.random.key(seed), 6)
    part_keys = jax.random.split(jax.random.fold_in(key_list[5], part), 6)
    return {
        "records": noise(part_keys[0], (C, TOTAL), 1.0, 6.0, ((1, 16),)),
        "bank": noise(part_keys[1], (BANK, C, L), 1.0, 6.0, ((0, 16),)),
        "plan": jax.random.randint(part_keys[2], (STEPS,), 0, N_TM).astype(jnp.int32),
        "template_ids": place_ends(jax.random.randint(part_keys[3], (STEPS, K), 0, SLOTS), jax.random.fold_in(part_keys[3], 1), 0, SLOTS - 1).astype(jnp.int32),
        "channel_mask": place_ends((jax.random.randint(part_keys[4], (C,), 0, 4) < 3).astype(jnp.int32), jax.random.fold_in(part_keys[4], 1), 0, 1),
    }


def correlate(extended, chosen, inv_norm, mask_f, scale):
    kcount, chans, taps = chosen.shape
    kernel = jnp.transpose(chosen, (1, 0, 2)).reshape(chans * kcount, 1, taps)
    raw = lax.conv_general_dilated(extended[None], kernel, (1,), 'VALID', dimension_numbers=('NCH', 'OIH', 'NCH'), feature_group_count=chans, preferred_element_type=jnp.float32)[0]
    raw = raw.reshape(chans, kcount, -1)
    chosen_f = chosen.astype(jnp.float32)
    weight = mask_f[None, :] / jnp.sqrt(lax.optimization_barrier(jnp.sum(chosen_f * chosen_f, axis=2)) + 1e-06)
    normed = raw * inv_norm[:, None, :]
    return scale * jnp.einsum('kc,ckt->kt', weight, normed, precision=lax.Precision.HIGHEST)

def reference(records, bank, plan, template_ids, channel_mask):
    taps = bank.shape[2]
    chans = records.shape[0]
    extended = jnp.concatenate([records, jnp.zeros((chans, taps - 1), records.dtype)], axis=1)
    sq = extended.astype(jnp.float32) ** 2
    energy = lax.reduce_window(sq, jnp.array(0.0, sq.dtype), lax.add, (1, taps), (1, 1), 'VALID')
    inv_norm = 1.0 / jnp.sqrt(energy + 1e-06)
    mask_f = channel_mask.astype(jnp.float32)
    scale = jnp.sqrt(taps / (1.0 + jnp.sum(mask_f)))

    def one_step(pair):
        owner, ids = pair
        rows = (owner * SLOTS + ids).astype(jnp.int32)
        chosen = jnp.take(bank, rows, axis=0)
        return correlate(extended, chosen, inv_norm, mask_f, scale)
    return lax.map(one_step, (plan, template_ids))
```

```python
import functools

import jax
import jax.numpy as jnp
from jax import lax
from jax.experimental import pallas as pl
from jax.experimental.pallas import tpu as pltpu
from jax.sharding import PartitionSpec as P

MESH = pl.DeviceIdType.MESH
LANES = 128


def up(value, unit):
    return -(-value // unit) * unit


def kernel(
    n, steps, kcount, taps,
    plan_ref, ids_ref, mask_s, mask_v, rec_ref, bank_ref, out_ref,
    wide, rwide, tsend, rsend, trecv, rrecv, xs, frames, inv, tmpl, wts, acc, osend, orecv,
    ts_sem, tr_sem, rs_sem, rr_sem, os_sem, or_sem,
):
    me = lax.axis_index("tm")
    templates = steps * kcount
    chans, block = rec_ref.shape
    own = chans // n
    halves = block // LANES
    width = frames.shape[2] // LANES

    barrier = pltpu.get_barrier_semaphore()

    @pl.loop(1, n)
    def _(o):
        pl.semaphore_signal(barrier, inc=1, device_id={"tm": lax.rem(me + o, n)}, device_id_type=MESH)

    rec_f = rec_ref[...].astype(jnp.float32)
    for v in range(halves):
        rwide[v] = rec_f[:, v * LANES : (v + 1) * LANES]
    pad = 2 * LANES - taps
    for s in range(steps):
        for k in range(kcount):
            row = (s * kcount + k) * chans
            pick = bank_ref[ids_ref[s, k]].astype(jnp.float32)
            pick = jnp.concatenate([pick, jnp.zeros((chans, pad), jnp.float32)], axis=1)
            for v in range(2):
                wide[v, row : row + chans, :] = pick[:, v * LANES : (v + 1) * LANES]

    @pl.loop(0, n)
    def _(d):
        for v in range(halves):
            rsend[d, :, v * LANES : (v + 1) * LANES] = rwide[v, pl.ds(d, own, stride=n), :].astype(jnp.bfloat16)
        for v in range(2):
            tsend[d, :, v * LANES : (v + 1) * LANES] = wide[v, pl.ds(d, templates * own, stride=n), :].astype(jnp.bfloat16)

    rrecv[me] = rsend[me]
    trecv[me] = tsend[me]

    def hop(send, recv, send_sem, recv_sem, o):
        to = lax.rem(me + o, n)
        return pltpu.make_async_remote_copy(
            src_ref=send.at[to],
            dst_ref=recv.at[me],
            send_sem=send_sem.at[o],
            recv_sem=recv_sem.at[o],
            device_id={"tm": to},
            device_id_type=MESH,
        )

    pl.semaphore_wait(barrier, n - 1)

    @pl.loop(1, n)
    def _(o):
        hop(rsend, rrecv, rs_sem, rr_sem, o).start()

    @pl.loop(1, n)
    def _(o):
        hop(tsend, trecv, ts_sem, tr_sem, o).start()

    @pl.loop(1, n)
    def _(o):
        hop(rsend, rrecv, rs_sem, rr_sem, o).wait()

    for v in range(halves):
        for a in range(n):
            xs[v, a * own : (a + 1) * own, :] = rrecv[a, :, v * LANES : (v + 1) * LANES].astype(jnp.float32)
        xs[v, n * own :, :] = jnp.zeros((xs.shape[1] - n * own, LANES), jnp.float32)
    shift = lax.broadcasted_iota(jnp.int32, (LANES, width * LANES), 1) - lax.broadcasted_iota(
        jnp.int32, (LANES, width * LANES), 0
    )
    band = jnp.where((shift >= 0) & (shift < taps), 1.0, 0.0).astype(jnp.bfloat16)
    live = jnp.sum(mask_v[...].astype(jnp.float32), axis=1, keepdims=True)
    scale = jnp.sqrt(taps / (1.0 + live))

    @pl.loop(0, own)
    def _(i):
        tiles = [
            xs[q % halves, pl.ds(i + (q // halves) * own, n, stride=own), :] for q in range(halves + width - 1)
        ]
        x = jnp.concatenate(
            [jnp.concatenate(tiles[h : h + width], axis=1) for h in range(halves)], axis=0
        )
        frames[i] = x.astype(jnp.bfloat16)
        sq = x * x
        high = sq.astype(jnp.bfloat16)
        low = (sq - high.astype(jnp.float32)).astype(jnp.bfloat16)
        dims = (((1,), (1,)), ((), ()))
        energy = lax.dot_general(high, band, dims, preferred_element_type=jnp.float32)
        energy += lax.dot_general(low, band, dims, preferred_element_type=jnp.float32)
        factor = scale * mask_s[i * n + me].astype(jnp.float32)
        inv[i] = factor / jnp.sqrt(energy + 1e-06)

    @pl.loop(1, n)
    def _(o):
        hop(tsend, trecv, ts_sem, tr_sem, o).wait()

    rows = kcount * own
    for s in range(steps):
        got = trecv[plan_ref[s]].astype(jnp.float32)[s * rows : (s + 1) * rows]
        tmpl[s * rows : (s + 1) * rows, : 2 * LANES] = got
        energy = jnp.sum(got * got, axis=1, keepdims=True)
        wts[s * rows : (s + 1) * rows, :] = jnp.broadcast_to(1.0 / jnp.sqrt(energy + 1e-06), (rows, LANES))
    if width > 2:
        tmpl[:, 2 * LANES :] = jnp.zeros((templates * own, (width - 2) * LANES), jnp.float32)
    acc[...] = jnp.zeros_like(acc)

    @pl.loop(0, own)
    def _(i):
        x = frames[i]
        norm = inv[i]
        for k in range(templates):
            row = k * own + i
            base = jnp.broadcast_to(tmpl[pl.ds(row, 1), :], (LANES, width * LANES))
            toeplitz = pltpu.roll(base, 0, 1, stride=1, stride_axis=0).astype(jnp.bfloat16)
            raw = lax.dot_general(x, toeplitz, (((1,), (1,)), ((), ())), preferred_element_type=jnp.float32)
            part = raw * norm * wts[pl.ds(row, 1), :]
            for h in range(halves):
                at = (h * templates + k) * n
                acc[at : at + n, :] += part[h * n : (h + 1) * n]

    @pl.loop(0, n)
    def _(d):
        osend[d] = acc[pl.ds(d, halves * templates, stride=n), :]

    @pl.loop(1, n)
    def _(o):
        hop(osend, orecv, os_sem, or_sem, o).start()

    total = osend[me]
    orecv[me] = total

    @pl.loop(1, n)
    def _(o):
        hop(osend, orecv, os_sem, or_sem, o).wait()

    final = jnp.sum(orecv[...], axis=0)
    for h in range(halves):
        for s in range(steps):
            at = h * templates + s * kcount
            out_ref[s, :, h * LANES : (h + 1) * LANES] = final[at : at + kcount]


def shards(records, bank, plan, template_ids, channel_mask):
    n = lax.axis_size("tm")
    steps, kcount = template_ids.shape
    chans, block = records.shape
    taps = bank.shape[2]
    own = chans // n
    templates = steps * kcount
    halves = block // LANES
    width = up(LANES + taps - 1, LANES) // LANES
    vmem = pl.BlockSpec(memory_space=pltpu.VMEM)
    smem = pl.BlockSpec(memory_space=pltpu.SMEM)
    f32, bf16 = jnp.float32, jnp.bfloat16
    dma = pltpu.SemaphoreType.DMA((n,))
    extra = -(-(halves + width - 2) // halves)
    return pl.pallas_call(
        functools.partial(kernel, n, steps, kcount, taps),
        out_shape=jax.ShapeDtypeStruct((steps, kcount, block), f32),
        in_specs=[smem, smem, smem, vmem, vmem, vmem],
        out_specs=vmem,
        scratch_shapes=[
            pltpu.VMEM((2, templates * chans, LANES), f32),
            pltpu.VMEM((halves, chans, LANES), f32),
            pltpu.VMEM((n, templates * own, 2 * LANES), bf16),
            pltpu.VMEM((n, own, block), bf16),
            pltpu.VMEM((n, templates * own, 2 * LANES), bf16),
            pltpu.VMEM((n, own, block), bf16),
            pltpu.VMEM((halves, (n + extra) * own, LANES), f32),
            pltpu.VMEM((own, halves * n, width * LANES), bf16),
            pltpu.VMEM((own, halves * n, LANES), f32),
            pltpu.VMEM((templates * own, width * LANES), f32),
            pltpu.VMEM((templates * own, LANES), f32),
            pltpu.VMEM((halves * templates * n, LANES), f32),
            pltpu.VMEM((n, halves * templates, LANES), f32),
            pltpu.VMEM((n, halves * templates, LANES), f32),
            dma, dma, dma, dma, dma, dma,
        ],
        compiler_params=pltpu.CompilerParams(
            collective_id=0, has_side_effects=True, vmem_limit_bytes=60 * 1024 * 1024
        ),
        name="detect",
    )(plan, template_ids, channel_mask, channel_mask.reshape(1, -1), records, bank)


def solution(mesh):
    placed = (
        P("groups", "tm"),
        P("tm", "groups", None),
        P("groups"),
        P("groups", None),
        P("groups"),
    )
    return jax.shard_map(
        shards, mesh=mesh, in_specs=placed, out_specs=P("groups", None, "tm"), check_vma=False
    )
```

```python
import functools

import jax
import jax.numpy as jnp
from jax import lax
from jax.experimental import pallas as pl
from jax.experimental.pallas import tpu as pltpu
from jax.sharding import PartitionSpec as P

MESH = pl.DeviceIdType.MESH
LANES = 128


def up(value, unit):
    return -(-value // unit) * unit


def kernel(
    n, steps, kcount, taps, unroll,
    plan_ref, ids_ref, mask_s, mask_v, rec_ref, bank_ref, out_ref,
    wide, rwide, tsend, tpart, tcomb, rsend, trecv, rrecv, xs, frames, inv, tmpl, wts, acc, osend, orecv,
    cs_sem, cr_sem, ts_sem, tr_sem, rs_sem, rr_sem, os_sem, or_sem,
):
    me = lax.axis_index("tm")
    chip, core = me // 2, me % 2
    chips = n // 2
    partner = me + 1 - 2 * core
    chans, block = rec_ref.shape
    own = chans // n
    rows = kcount * own
    halves = block // LANES
    width = frames.shape[2] // LANES
    dims = (((1,), (1,)), ((), ()))

    barrier = pltpu.get_barrier_semaphore()

    @pl.loop(1, n)
    def _(o):
        pl.semaphore_signal(barrier, inc=1, device_id={"tm": lax.rem(me + o, n)}, device_id_type=MESH)

    rec_f = rec_ref[...].astype(jnp.float32)
    for v in range(halves):
        rwide[v] = rec_f[:, v * LANES : (v + 1) * LANES]
    pad = 2 * LANES - taps
    for s in range(steps):
        for k in range(kcount):
            pick = bank_ref[ids_ref[s, k]].astype(jnp.float32)
            pick = jnp.concatenate([pick, jnp.zeros((chans, pad), jnp.float32)], axis=1)
            for v in range(2):
                wide[s, v, k * chans : (k + 1) * chans, :] = pick[:, v * LANES : (v + 1) * LANES]

    @pl.loop(0, n)
    def _(d):
        for v in range(halves):
            rsend[d, :, v * LANES : (v + 1) * LANES] = rwide[v, pl.ds(d, own, stride=n), :].astype(jnp.bfloat16)
        for s in range(steps):
            for v in range(2):
                tsend[s, d % 2, d // 2, :, v * LANES : (v + 1) * LANES] = wide[
                    s, v, pl.ds(d, rows, stride=n), :
                ].astype(jnp.bfloat16)

    rrecv[me] = rsend[me]

    def hop(send, recv, send_sem, recv_sem, o):
        to = lax.rem(me + o, n)
        return pltpu.make_async_remote_copy(
            src_ref=send.at[to], dst_ref=recv.at[me], send_sem=send_sem.at[o], recv_sem=recv_sem.at[o],
            device_id={"tm": to}, device_id_type=MESH,
        )

    def across(s):
        return pltpu.make_async_remote_copy(
            src_ref=tsend.at[s, 1 - core], dst_ref=tpart.at[s], send_sem=cs_sem.at[s], recv_sem=cr_sem.at[s],
            device_id={"tm": partner}, device_id_type=MESH,
        )

    def spread(s, o):
        to = lax.rem(chip + o, chips)
        return pltpu.make_async_remote_copy(
            src_ref=tcomb.at[s, to], dst_ref=trecv[s].at[chip], send_sem=ts_sem.at[s, o], recv_sem=tr_sem.at[s, o],
            device_id={"tm": 2 * to + core}, device_id_type=MESH,
        )

    pl.semaphore_wait(barrier, n - 1)
    for s in range(steps):
        across(s).start()

    @pl.loop(1, n)
    def _(o):
        hop(rsend, rrecv, rs_sem, rr_sem, o).start()

    for s in range(steps):
        across(s).wait_recv()
        theirs = plan_ref[s] == partner
        mix = jnp.where(theirs, tpart[s].astype(jnp.float32), tsend[s, core].astype(jnp.float32))
        tcomb[s] = mix.astype(jnp.bfloat16)
        trecv[s][chip] = tcomb[s, chip]

        @pl.loop(1, chips)
        def _(o):
            spread(s, o).start()

    @pl.loop(1, n)
    def _(o):
        hop(rsend, rrecv, rs_sem, rr_sem, o).wait_recv()

    for v in range(halves):
        for a in range(n):
            xs[v, a * own : (a + 1) * own, :] = rrecv[a, :, v * LANES : (v + 1) * LANES].astype(jnp.float32)
        xs[v, n * own :, :] = jnp.zeros((xs.shape[1] - n * own, LANES), jnp.float32)
    shift = lax.broadcasted_iota(jnp.int32, (LANES, width * LANES), 1) - lax.broadcasted_iota(
        jnp.int32, (LANES, width * LANES), 0
    )
    band = jnp.where((shift >= 0) & (shift < taps), 1.0, 0.0).astype(jnp.bfloat16)
    live = jnp.sum(mask_v[...].astype(jnp.float32), axis=1, keepdims=True)
    scale = jnp.sqrt(taps / (1.0 + live))

    def frame(i, carry):
        tiles = [
            xs[q % halves, pl.ds(i + (q // halves) * own, n, stride=own), :] for q in range(halves + width - 1)
        ]
        x = jnp.concatenate(
            [jnp.concatenate(tiles[h : h + width], axis=1) for h in range(halves)], axis=0
        )
        frames[i] = x.astype(jnp.bfloat16)
        sq = x * x
        high = sq.astype(jnp.bfloat16)
        low = (sq - high.astype(jnp.float32)).astype(jnp.bfloat16)
        energy = lax.dot_general(
            jnp.concatenate([high, low], axis=0), band, dims, preferred_element_type=jnp.float32
        )
        energy = energy[: halves * n] + energy[halves * n :]
        factor = scale * mask_s[i * n + me].astype(jnp.float32)
        inv[i] = factor / jnp.sqrt(energy + 1e-06)
        return carry

    lax.fori_loop(0, own, frame, 0, unroll=unroll)
    if width > 2:
        tmpl[:, 2 * LANES :] = jnp.zeros((rows, (width - 2) * LANES), jnp.float32)

    for s in range(steps):

        @pl.loop(1, chips)
        def _(o):
            spread(s, o).wait_recv()

        got = trecv[s][lax.div(plan_ref[s], 2)].astype(jnp.float32)
        tmpl[:, : 2 * LANES] = got
        energy = jnp.sum(got * got, axis=1, keepdims=True)
        wts[...] = jnp.broadcast_to(1.0 / jnp.sqrt(energy + 1e-06), (rows, LANES))
        acc[s] = jnp.zeros(acc.shape[1:], jnp.float32)

        def channel(i, carry):
            banks = []
            for k in range(kcount):
                base = jnp.broadcast_to(tmpl[pl.ds(k * own + i, 1), :], (16, width * LANES)).astype(jnp.bfloat16)
                base = jnp.concatenate([base] * (LANES // 16), axis=0)
                banks.append(pltpu.roll(base, 0, 1, stride=1, stride_axis=0))
            raw = lax.dot_general(
                frames[i], jnp.concatenate(banks, axis=0), dims, preferred_element_type=jnp.float32
            )
            norm = inv[i]
            for k in range(kcount):
                part = raw[:, k * LANES : (k + 1) * LANES] * norm * wts[pl.ds(k * own + i, 1), :]
                for h in range(halves):
                    at = (h * kcount + k) * n
                    acc[s, at : at + n, :] += part[h * n : (h + 1) * n]
            return carry

        lax.fori_loop(0, own, channel, 0, unroll=unroll)

        for d in range(n):
            osend[s, d] = acc[s, pl.ds(d, halves * kcount, stride=n), :]
        orecv[s, me] = osend[s, me]

        @pl.loop(1, n)
        def _(o):
            hop(osend.at[s], orecv.at[s], os_sem.at[s], or_sem.at[s], o).start()

    for s in range(steps):

        @pl.loop(1, n)
        def _(o):
            hop(osend.at[s], orecv.at[s], os_sem.at[s], or_sem.at[s], o).wait_recv()

        final = jnp.sum(orecv[s], axis=0)
        for h in range(halves):
            out_ref[s, :, h * LANES : (h + 1) * LANES] = final[h * kcount : (h + 1) * kcount]

    for s in range(steps):
        across(s).wait_send()

        @pl.loop(1, chips)
        def _(o):
            spread(s, o).wait_send()

        @pl.loop(1, n)
        def _(o):
            hop(osend.at[s], orecv.at[s], os_sem.at[s], or_sem.at[s], o).wait_send()

    @pl.loop(1, n)
    def _(o):
        hop(rsend, rrecv, rs_sem, rr_sem, o).wait_send()


def shards(records, bank, plan, template_ids, channel_mask):
    n = lax.axis_size("tm")
    steps, kcount = template_ids.shape
    chans, block = records.shape
    taps = bank.shape[2]
    own = chans // n
    rows = kcount * own
    halves = block // LANES
    width = up(LANES + taps - 1, LANES) // LANES
    vmem = pl.BlockSpec(memory_space=pltpu.VMEM)
    smem = pl.BlockSpec(memory_space=pltpu.SMEM)
    f32, bf16 = jnp.float32, jnp.bfloat16
    dma = pltpu.SemaphoreType.DMA
    extra = -(-(halves + width - 2) // halves)
    return pl.pallas_call(
        functools.partial(kernel, n, steps, kcount, taps, min(own, 4)),
        out_shape=jax.ShapeDtypeStruct((steps, kcount, block), f32),
        in_specs=[smem, smem, smem, vmem, vmem, vmem],
        out_specs=vmem,
        scratch_shapes=[
            pltpu.VMEM((steps, 2, kcount * chans, LANES), f32),
            pltpu.VMEM((halves, chans, LANES), f32),
            pltpu.VMEM((steps, 2, n // 2, rows, 2 * LANES), bf16),
            pltpu.VMEM((steps, n // 2, rows, 2 * LANES), bf16),
            pltpu.VMEM((steps, n // 2, rows, 2 * LANES), bf16),
            pltpu.VMEM((n, own, block), bf16),
            [pltpu.VMEM((n // 2, rows, 2 * LANES), bf16)] * steps,
            pltpu.VMEM((n, own, block), bf16),
            pltpu.VMEM((halves, (n + extra) * own, LANES), f32),
            pltpu.VMEM((own, halves * n, width * LANES), bf16),
            pltpu.VMEM((own, halves * n, LANES), f32),
            pltpu.VMEM((rows, width * LANES), f32),
            pltpu.VMEM((rows, LANES), f32),
            pltpu.VMEM((steps, halves * kcount * n, LANES), f32),
            pltpu.VMEM((steps, n, halves * kcount, LANES), f32),
            pltpu.VMEM((steps, n, halves * kcount, LANES), f32),
            dma((steps,)), dma((steps,)), dma((steps, n // 2)), dma((steps, n // 2)),
            dma((n,)), dma((n,)), dma((steps, n)), dma((steps, n)),
        ],
        compiler_params=pltpu.CompilerParams(
            collective_id=0, has_side_effects=True, vmem_limit_bytes=60 * 1024 * 1024
        ),
        name="detect",
    )(plan, template_ids, channel_mask, channel_mask.reshape(1, -1), records, bank)


def solution(mesh):
    placed = (
        P("groups", "tm"),
        P("tm", "groups", None),
        P("groups"),
        P("groups", None),
        P("groups"),
    )
    return jax.shard_map(
        shards, mesh=mesh, in_specs=placed, out_specs=P("groups", None, "tm"), check_vma=False
    )
```

```python
import functools

import jax
import jax.numpy as jnp
from jax import lax
from jax.experimental import pallas as pl
from jax.experimental.pallas import tpu as pltpu
from jax.sharding import PartitionSpec as P

MESH = pl.DeviceIdType.MESH
LANES = 128


def up(value, unit):
    return -(-value // unit) * unit


def kernel(
    n, steps, kcount, taps, unroll,
    plan_ref, ids_ref, mask_s, mask_v, rec_ref, bank_ref, out_ref,
    wide, rwide, tsend, tpart, tcomb, rsend, trecv, rrecv, xs, frames, inv, tmpl, wts, acc, osend, orecv, bank_v,
    bank_sem, cs_sem, cr_sem, ts_sem, tr_sem, rs_sem, rr_sem, os_sem, or_sem,
):
    me = lax.axis_index("tm")
    chip, core = me // 2, me % 2
    chips = n // 2
    partner = me + 1 - 2 * core
    chans, block = rec_ref.shape
    own = chans // n
    rows = kcount * own
    halves = block // LANES
    width = frames.shape[2] // LANES
    dims = (((1,), (1,)), ((), ()))

    barrier = pltpu.get_barrier_semaphore()

    @pl.loop(1, n)
    def _(o):
        pl.semaphore_signal(barrier, inc=1, device_id={"tm": lax.rem(me + o, n)}, device_id_type=MESH)

    fetch = pltpu.make_async_copy(bank_ref, bank_v, bank_sem)
    fetch.start()

    rec_f = rec_ref[...].astype(jnp.float32)
    for v in range(halves):
        rwide[v] = rec_f[:, v * LANES : (v + 1) * LANES]
    pad = 2 * LANES - taps
    fetch.wait()
    for s in range(steps):
        for k in range(kcount):
            pick = bank_v[ids_ref[k, s]].astype(jnp.float32)
            pick = jnp.concatenate([pick, jnp.zeros((chans, pad), jnp.float32)], axis=1)
            for v in range(2):
                wide[s, v, k * chans : (k + 1) * chans, :] = pick[:, v * LANES : (v + 1) * LANES]

    @pl.loop(0, n)
    def _(d):
        for v in range(halves):
            rsend[d, :, v * LANES : (v + 1) * LANES] = rwide[v, pl.ds(d, own, stride=n), :].astype(jnp.bfloat16)
        for s in range(steps):
            for v in range(2):
                tsend[s, d % 2, d // 2, :, v * LANES : (v + 1) * LANES] = wide[
                    s, v, pl.ds(d, rows, stride=n), :
                ].astype(jnp.bfloat16)

    rrecv[me] = rsend[me]

    def hop(send, recv, send_sem, recv_sem, o):
        to = lax.rem(me + o, n)
        return pltpu.make_async_remote_copy(
            src_ref=send.at[to], dst_ref=recv.at[me], send_sem=send_sem.at[o], recv_sem=recv_sem.at[o],
            device_id={"tm": to}, device_id_type=MESH,
        )

    def across(s):
        return pltpu.make_async_remote_copy(
            src_ref=tsend.at[s, 1 - core], dst_ref=tpart.at[s], send_sem=cs_sem.at[s], recv_sem=cr_sem.at[s],
            device_id={"tm": partner}, device_id_type=MESH,
        )

    def spread(s, o):
        to = lax.rem(chip + o, chips)
        return pltpu.make_async_remote_copy(
            src_ref=tcomb.at[s, to], dst_ref=trecv[s].at[chip], send_sem=ts_sem.at[s, o], recv_sem=tr_sem.at[s, o],
            device_id={"tm": 2 * to + core}, device_id_type=MESH,
        )

    pl.semaphore_wait(barrier, n - 1)
    for s in range(steps):
        across(s).start()

    @pl.loop(1, n)
    def _(o):
        hop(rsend, rrecv, rs_sem, rr_sem, o).start()

    for s in range(steps):
        across(s).wait_recv()
        theirs = plan_ref[s] == partner
        mix = jnp.where(theirs, tpart[s].astype(jnp.float32), tsend[s, core].astype(jnp.float32))
        tcomb[s] = mix.astype(jnp.bfloat16)
        trecv[s][chip] = tcomb[s, chip]

        @pl.loop(1, chips)
        def _(o):
            spread(s, lax.rem(o + chips // 2 - 1, chips - 1) + 1).start()

    @pl.loop(1, n)
    def _(o):
        hop(rsend, rrecv, rs_sem, rr_sem, o).wait_recv()

    for v in range(halves):
        for a in range(n):
            xs[v, a * own : (a + 1) * own, :] = rrecv[a, :, v * LANES : (v + 1) * LANES].astype(jnp.float32)
        xs[v, n * own :, :] = jnp.zeros((xs.shape[1] - n * own, LANES), jnp.float32)
    shift = lax.broadcasted_iota(jnp.int32, (LANES, width * LANES), 1) - lax.broadcasted_iota(
        jnp.int32, (LANES, width * LANES), 0
    )
    band = jnp.where((shift >= 0) & (shift < taps), 1.0, 0.0).astype(jnp.bfloat16)
    live = jnp.sum(mask_v[...].astype(jnp.float32), axis=1, keepdims=True)
    scale = jnp.sqrt(taps / (1.0 + live))

    def frame(i, carry):
        tiles = [
            xs[q % halves, pl.ds(i + (q // halves) * own, n, stride=own), :] for q in range(halves + width - 1)
        ]
        x = jnp.concatenate(
            [jnp.concatenate(tiles[h : h + width], axis=1) for h in range(halves)], axis=0
        )
        frames[i] = x.astype(jnp.bfloat16)
        sq = x * x
        high = sq.astype(jnp.bfloat16)
        low = (sq - high.astype(jnp.float32)).astype(jnp.bfloat16)
        energy = lax.dot_general(
            jnp.concatenate([high, low], axis=0), band, dims, preferred_element_type=jnp.float32
        )
        energy = energy[: halves * n] + energy[halves * n :]
        factor = scale * mask_s[i * n + me].astype(jnp.float32)
        inv[i] = factor / jnp.sqrt(energy + 1e-06)
        return carry

    lax.fori_loop(0, own, frame, 0, unroll=unroll)
    if width > 2:
        tmpl[:, 2 * LANES :] = jnp.zeros((rows, (width - 2) * LANES), jnp.float32)

    for s in range(steps):

        @pl.loop(1, chips)
        def _(o):
            spread(s, o).wait_recv()

        got = trecv[s][lax.div(plan_ref[s], 2)].astype(jnp.float32)
        tmpl[:, : 2 * LANES] = got
        energy = jnp.sum(got * got, axis=1, keepdims=True)
        wts[...] = jnp.broadcast_to(1.0 / jnp.sqrt(energy + 1e-06), (rows, LANES))
        acc[s] = jnp.zeros(acc.shape[1:], jnp.float32)

        def channel(i, carry):
            banks = []
            for k in range(kcount):
                base = jnp.broadcast_to(tmpl[pl.ds(k * own + i, 1), :], (16, width * LANES)).astype(jnp.bfloat16)
                base = jnp.concatenate([base] * (LANES // 16), axis=0)
                banks.append(pltpu.roll(base, 0, 1, stride=1, stride_axis=0))
            raw = lax.dot_general(
                frames[i], jnp.concatenate(banks, axis=0), dims, preferred_element_type=jnp.float32
            )
            norm = inv[i]
            for k in range(kcount):
                part = raw[:, k * LANES : (k + 1) * LANES] * norm * wts[pl.ds(k * own + i, 1), :]
                for h in range(halves):
                    at = (h * kcount + k) * n
                    acc[s, at : at + n, :] += part[h * n : (h + 1) * n]
            return carry

        lax.fori_loop(0, own, channel, 0, unroll=unroll)

        for d in range(n):
            osend[s, d] = acc[s, pl.ds(d, halves * kcount, stride=n), :]
        orecv[s, me] = osend[s, me]

        @pl.loop(1, n)
        def _(o):
            hop(osend.at[s], orecv.at[s], os_sem.at[s], or_sem.at[s], o).start()

    for s in range(steps):

        @pl.loop(1, n)
        def _(o):
            hop(osend.at[s], orecv.at[s], os_sem.at[s], or_sem.at[s], o).wait_recv()

        final = jnp.sum(orecv[s], axis=0)
        for h in range(halves):
            out_ref[s, :, h * LANES : (h + 1) * LANES] = final[h * kcount : (h + 1) * kcount]

    for s in range(steps):
        across(s).wait_send()

        @pl.loop(1, chips)
        def _(o):
            spread(s, o).wait_send()

        @pl.loop(1, n)
        def _(o):
            hop(osend.at[s], orecv.at[s], os_sem.at[s], or_sem.at[s], o).wait_send()

    @pl.loop(1, n)
    def _(o):
        hop(rsend, rrecv, rs_sem, rr_sem, o).wait_send()


def shards(records, bank, plan, template_ids, channel_mask):
    n = lax.axis_size("tm")
    steps, kcount = template_ids.shape
    chans, block = records.shape
    taps = bank.shape[2]
    own = chans // n
    rows = kcount * own
    halves = block // LANES
    width = up(LANES + taps - 1, LANES) // LANES
    vmem = pl.BlockSpec(memory_space=pltpu.VMEM)
    smem = pl.BlockSpec(memory_space=pltpu.SMEM)
    f32, bf16 = jnp.float32, jnp.bfloat16
    dma = pltpu.SemaphoreType.DMA
    extra = -(-(halves + width - 2) // halves)
    return pl.pallas_call(
        functools.partial(kernel, n, steps, kcount, taps, own),
        out_shape=jax.ShapeDtypeStruct((steps, kcount, block), f32),
        in_specs=[smem, smem, smem, vmem, vmem, pl.BlockSpec(memory_space=pl.ANY)],
        out_specs=vmem,
        scratch_shapes=[
            pltpu.VMEM((steps, 2, kcount * chans, LANES), f32),
            pltpu.VMEM((halves, chans, LANES), f32),
            pltpu.VMEM((steps, 2, n // 2, rows, 2 * LANES), bf16),
            pltpu.VMEM((steps, n // 2, rows, 2 * LANES), bf16),
            pltpu.VMEM((steps, n // 2, rows, 2 * LANES), bf16),
            pltpu.VMEM((n, own, block), bf16),
            [pltpu.VMEM((n // 2, rows, 2 * LANES), bf16)] * steps,
            pltpu.VMEM((n, own, block), bf16),
            pltpu.VMEM((halves, (n + extra) * own, LANES), f32),
            pltpu.VMEM((own, halves * n, width * LANES), bf16),
            pltpu.VMEM((own, halves * n, LANES), f32),
            pltpu.VMEM((rows, width * LANES), f32),
            pltpu.VMEM((rows, LANES), f32),
            pltpu.VMEM((steps, halves * kcount * n, LANES), f32),
            pltpu.VMEM((steps, n, halves * kcount, LANES), f32),
            pltpu.VMEM((steps, n, halves * kcount, LANES), f32),
            pltpu.VMEM(bank.shape, bf16),
            dma(()), dma((steps,)), dma((steps,)), dma((steps, n // 2)), dma((steps, n // 2)),
            dma((n,)), dma((n,)), dma((steps, n)), dma((steps, n)),
        ],
        compiler_params=pltpu.CompilerParams(
            collective_id=0, has_side_effects=True, vmem_limit_bytes=60 * 1024 * 1024
        ),
        name="detect",
    )(plan, template_ids.T, channel_mask, channel_mask.reshape(1, -1), records, bank)


def solution(mesh):
    placed = (
        P("groups", "tm"),
        P("tm", "groups", None),
        P("groups"),
        P("groups", None),
        P("groups"),
    )
    return jax.shard_map(
        shards, mesh=mesh, in_specs=placed, out_specs=P("groups", None, "tm"), check_vma=False
    )
```
